512 devices in a mesh: scen: 8 (over x, y_hi), grid: 64 (over y_lo, z, core).
Axes of the slice: x: 4, y: 8 (y_hi: 2, y_lo: 4; y = y_hi * 4 + y_lo), z: 8, core: 2. Of those that a mesh axis runs over, the one named last changes fastest.
Arguments:
- forward_states: float32 [8, 4, 64, 256, 512], P('scen', None, 'grid'), may hold values from -6 to 6
- kappa: float32 [64, 256, 512], P('grid'), may hold values from 0.02 to 0.08
- courant: float32 [64, 256, 512], P('grid'), may hold values from 0.1 to 0.45
- direction: float32 [64, 256, 512], P('grid'), may hold values from -6 to 6
- obs_index: int32 [8, 262144], P('scen', 'grid'), may hold values from 0 to 131071
- obs_weight: float32 [8, 262144], P('scen', 'grid'), may hold values from 0.5 to 4
Outputs:
- hess_vec: float32 [64, 256, 512], P('grid', 'scen')
The draws below stay inside these ranges and needn't reach their ends.
Inputs may be any that keep to these rules, and one draw needn't show every extreme that they name: `obs_index`: an index names a cell of the slab of 1 x 256 x 512 cells that belongs to its block of 4096 observations.
All inputs are finite; a program needn't handle non-finite values.
Results may differ from the reference program's by a relative error of at most 0.00002.
Values sent between devices are 32-bit elements; how exact they have to be, the bound alone decides.
No kernel may reach another device: no remote copies, remote signals or barrier semaphores. Data moves between devices by JAX's collectives and lax.ppermute only.
A program may use at most 64 MiB of HBM per device.

```python
import math
import jax
import jax.numpy as jnp

CX = 1
NY = 256
NZ = 512
OBS_DEV = 4096
STEPS = 4
SCENS = 8
NX = 64
OBS = 262144


def plant(result, own_key, low, top_value):
    dims = result.shape
    place = [jax.random.randint(jax.random.fold_in(own_key, axis), (), 0, dims[axis]) for axis in range(len(dims))]
    result = result.at[tuple(place)].set(low)
    longest = dims.index(max(dims))
    place[longest] = (place[longest] + 1) % dims[longest]
    return result.at[tuple(place)].set(top_value)


def block_scale(rng, dims, shards, least, high):
    loudness, own = 1.0, jax.random.fold_in(rng, 6)
    for position, shards_of in shards:
        draws = jnp.exp(jax.random.uniform(jax.random.fold_in(own, position), (shards_of,), jnp.float32, least / len(shards), high / len(shards)))
        loudness = loudness * jnp.repeat(draws, dims[position] // shards_of).reshape([-1 if axis == position else 1 for axis in range(len(dims))])
    return loudness


def bell_draw(stream_key, dims, scale, limit, cuts=(), held_as=jnp.bfloat16):
    entries = scale * jax.random.normal(stream_key, dims, jnp.float32)
    if cuts:
        entries = entries * block_scale(stream_key, dims, cuts, -0.22, 0.18)
    return jnp.clip(entries, -limit, limit).astype(held_as)


def setup_inputs(seed: int = 0) -> dict:
    splits = jax.random.split(jax.random.key(seed), 7)
    return {
        "forward_states": bell_draw(splits[0], (SCENS, STEPS, NX, NY, NZ), 1.0, 6.0, ((0, 8), (2, 64)), jnp.float32),
        "kappa": jnp.clip(jnp.exp(math.log(0.08) - 1.3862944 * jax.random.uniform(splits[1], (NX, NY, NZ), jnp.float32) ** block_scale(splits[1], (NX, NY, NZ), ((0, 64),), -0.2, 0.2)), 0.02, 0.08),
        "courant": jnp.clip(0.1 + 0.35 * jax.random.uniform(splits[2], (NX, NY, NZ), jnp.float32) ** block_scale(splits[2], (NX, NY, NZ), ((0, 64),), -0.2, 0.2), 0.1, 0.45),
        "direction": bell_draw(splits[3], (NX, NY, NZ), 1.0, 6.0, ((0, 64),), jnp.float32),
        "obs_index": plant(jax.random.randint(splits[4], (SCENS, OBS), 0, CX * NY * NZ), jax.random.fold_in(splits[4], 1), 0, (CX * NY * NZ) - 1).astype(jnp.int32),
        "obs_weight": jnp.clip(jnp.exp(math.log(4.0) - 2.0794415 * jax.random.uniform(splits[5], (SCENS, OBS), jnp.float32) ** block_scale(splits[5], (SCENS, OBS), ((0, 8), (1, 64)), -0.2, 0.2)), 0.5, 4.0),
    }


source_gain = 0.2
prior_gain = 0.5
prior_reach = 0.1


def laplace(padded):
    inner = padded[..., 1:-1, :, :]
    widths = [(0, 0)] * (inner.ndim - 2) + [(1, 1), (1, 1)]
    side = jnp.pad(inner, widths)
    total = padded[..., 2:, :, :] + padded[..., :-2, :, :]
    total = total + side[..., 2:, 1:-1] + side[..., :-2, 1:-1]
    total = total + side[..., 1:-1, 2:] + side[..., 1:-1, :-2]
    return total - 6.0 * inner


def pad_first(field):
    widths = [(0, 0)] * (field.ndim - 3) + [(1, 1), (0, 0), (0, 0)]
    return jnp.pad(field, widths)


def reference(forward_states, kappa, courant, direction, obs_index, obs_weight):
    cells = CX * NY * NZ
    shape = direction.shape
    total = jnp.zeros(shape, jnp.float32)
    block = (jnp.arange(OBS, dtype=jnp.int32) // OBS_DEV).astype(jnp.int32)
    for scenario in range(SCENS):
        lap_states = laplace(pad_first(forward_states[scenario]))
        tangent = source_gain * direction * lap_states[0]
        for step in range(1, STEPS):
            padded = pad_first(tangent)
            tangent = tangent + kappa * laplace(padded) - courant * (tangent - padded[:-2]) + source_gain * direction * lap_states[step]
        flat = (block * cells + obs_index[scenario]).astype(jnp.int32)
        values = tangent.reshape(-1)[flat] * obs_weight[scenario]
        adjoint = jnp.zeros((NX * NY * NZ,), jnp.float32).at[flat].add(values).reshape(shape)
        partial_value = source_gain * lap_states[STEPS - 1] * adjoint
        for step in range(STEPS - 2, -1, -1):
            weighted = pad_first(kappa * adjoint)
            carried = pad_first(courant * adjoint)
            adjoint = adjoint + laplace(weighted) - (courant * adjoint - carried[2:])
            partial_value = partial_value + source_gain * lap_states[step] * adjoint
        total = total + partial_value
    prior = prior_gain * (direction - prior_reach * laplace(pad_first(direction)))
    return total + prior
```

```python
import jax
import jax.numpy as jnp
from jax import lax
from jax.experimental import pallas as pl
from jax.experimental.pallas import tpu as pltpu
from jax.sharding import PartitionSpec as P

source_gain = 0.2
prior_gain = 0.5
prior_reach = 0.1


def weight_kernel(index_ref, weight_ref, field_ref):
    rows, columns = field_ref.shape
    chunk = index_ref.shape[1]

    @pl.when(pl.program_id(0) == 0)
    def _():
        field_ref[...] = jnp.zeros_like(field_ref)

    index = index_ref[...]
    row = index // columns
    column = index - row * columns
    left = weight_ref[...]
    row_hit = lax.broadcasted_iota(jnp.int32, (rows, chunk), 0) == row
    column_hit = lax.broadcasted_iota(jnp.int32, (columns, chunk), 0) == column
    column_one = jnp.where(column_hit, 1.0, 0.0).astype(jnp.bfloat16)
    for _ in range(3):
        part = left.astype(jnp.bfloat16).astype(jnp.float32)
        left = left - part
        row_part = jnp.where(row_hit, part, 0.0).astype(jnp.bfloat16)
        field_ref[...] += lax.dot_general(
            row_part, column_one, (((1,), (1,)), ((), ())), preferred_element_type=jnp.float32
        )


def weight_field(index, weight, rows, columns):
    count = index.shape[1]
    chunk = 1024
    return pl.pallas_call(
        weight_kernel,
        grid=(count // chunk,),
        in_specs=[pl.BlockSpec((1, chunk), lambda i: (0, i))] * 2,
        out_specs=pl.BlockSpec((rows, columns), lambda i: (0, 0)),
        out_shape=jax.ShapeDtypeStruct((rows, columns), jnp.float32),
        compiler_params=pltpu.CompilerParams(vmem_limit_bytes=24 << 20),
        cost_estimate=pl.CostEstimate(
            flops=6 * rows * columns * count, bytes_accessed=4 * rows * columns, transcendentals=0
        ),
        name="weight_field",
    )(index, weight)


def side_sum(field):
    wide = jnp.pad(field, [(0, 0)] * (field.ndim - 2) + [(1, 1), (1, 1)])
    total = wide[..., 2:, 1:-1] + wide[..., :-2, 1:-1]
    return total + wide[..., 1:-1, 2:] + wide[..., 1:-1, :-2] - 6.0 * field


def local(forward_states, kappa, courant, direction, obs_index, obs_weight):
    states = forward_states[0, :, 0]
    kappa, courant, direction = kappa[0], courant[0], direction[0]
    steps, rows, columns = states.shape
    slabs = lax.axis_size("grid")
    scens = lax.axis_size("scen")
    even = lax.axis_index("grid") % 2 == 0
    mine = lax.axis_index("scen")

    near = [(g, g ^ 1) for g in range(slabs)]
    far = [(g, g - 1 if g % 2 == 0 else g + 1) for g in range(slabs)]
    far = [(g, h) for g, h in far if 0 <= h < slabs]

    def swap(far_field, near_field):
        return lax.ppermute(far_field, "grid", far), lax.ppermute(near_field, "grid", near)

    fars, nears = [], lax.ppermute(states, "grid", near)
    for step in range(steps):
        fars.append(lax.ppermute(states[step], "grid", far))
    laps = [fars[k] + nears[k] + side_sum(states[k]) for k in range(steps)]

    weights = weight_field(obs_index, obs_weight, rows, columns)

    tangent = source_gain * direction * laps[0]
    for step in range(1, steps):
        over, beside = swap(tangent, tangent)
        below = jnp.where(even, over, beside)
        tangent = (
            tangent
            + kappa * (over + beside + side_sum(tangent))
            - courant * (tangent - below)
            + source_gain * direction * laps[step]
        )

    adjoint = tangent * weights
    partial_value = source_gain * laps[steps - 1] * adjoint
    for step in range(steps - 2, -1, -1):
        weighted = kappa * adjoint
        carried = courant * adjoint
        both = weighted + carried
        over, beside = swap(
            jnp.where(even, both, weighted), jnp.where(even, weighted, both)
        )
        adjoint = adjoint + (over + beside + side_sum(weighted)) - carried
        partial_value = partial_value + source_gain * laps[step] * adjoint

    share = rows // scens
    block = 2 * share
    blocks = scens // 2
    place, half = mine // 2, mine % 2
    arrived = []
    for hop in (2, 1, 3):
        piece = lax.dynamic_slice_in_dim(
            partial_value, ((place + hop) % blocks) * block, block, 0
        )
        ring = [(s, (s // 2 + hop) % blocks * 2 + s % 2) for s in range(scens)]
        arrived.append(lax.ppermute(piece, "scen", ring))
    total = lax.dynamic_slice_in_dim(partial_value, place * block, block, 0)
    for piece in arrived:
        total = total + piece
    other = lax.dynamic_slice_in_dim(total, (1 - half) * share, share, 0)
    kept = lax.dynamic_slice_in_dim(total, half * share, share, 0)
    across = lax.ppermute(other, "scen", [(s, s ^ 1) for s in range(scens)])

    own = lax.dynamic_slice_in_dim(direction, mine * share, share, 0)
    over, beside = swap(own, own)
    tall = jnp.pad(direction, ((1, 1), (0, 0)))
    tall = lax.dynamic_slice_in_dim(tall, mine * share, share + 2, 0)
    lap = over + beside + side_sum(tall)[1:-1]
    prior = prior_gain * (own - prior_reach * lap)
    return (kept + across + prior)[None]


def solution(mesh):
    return jax.shard_map(
        local,
        mesh=mesh,
        in_specs=(
            P("scen", None, "grid", None, None),
            P("grid", None, None),
            P("grid", None, None),
            P("grid", None, None),
            P("scen", "grid"),
            P("scen", "grid"),
        ),
        out_specs=P("grid", "scen", None),
        check_vma=False,
    )
```

```python
import jax
import jax.numpy as jnp
from jax import lax
from jax.experimental import pallas as pl
from jax.experimental.pallas import tpu as pltpu
from jax.sharding import PartitionSpec as P


source_gain = 0.2
prior_gain = 0.5
prior_reach = 0.1


def weight_kernel(index_ref, weight_ref, field_ref):
    rows, columns = field_ref.shape
    chunk = index_ref.shape[1]

    @pl.when(pl.program_id(0) == 0)
    def _():
        field_ref[...] = jnp.zeros_like(field_ref)

    index = index_ref[...]
    row = index // columns
    column = index - row * columns
    left = weight_ref[...]
    row_hit = lax.broadcasted_iota(jnp.int32, (rows, chunk), 0) == row
    column_hit = lax.broadcasted_iota(jnp.int32, (columns, chunk), 0) == column
    column_one = jnp.where(column_hit, 1.0, 0.0).astype(jnp.bfloat16)
    for _ in range(3):
        part = left.astype(jnp.bfloat16).astype(jnp.float32)
        left = left - part
        row_part = jnp.where(row_hit, part, 0.0).astype(jnp.bfloat16)
        field_ref[...] += lax.dot_general(
            row_part, column_one, (((1,), (1,)), ((), ())), preferred_element_type=jnp.float32
        )


def weight_field(index, weight, rows, columns):
    count = index.shape[1]
    chunk = 1024
    return pl.pallas_call(
        weight_kernel,
        grid=(count // chunk,),
        in_specs=[pl.BlockSpec((1, chunk), lambda i: (0, i))] * 2,
        out_specs=pl.BlockSpec((rows, columns), lambda i: (0, 0)),
        out_shape=jax.ShapeDtypeStruct((rows, columns), jnp.float32),
        compiler_params=pltpu.CompilerParams(vmem_limit_bytes=24 << 20),
        cost_estimate=pl.CostEstimate(
            flops=6 * rows * columns * count, bytes_accessed=4 * rows * columns, transcendentals=0
        ),
        name="weight_field",
    )(index, weight)


def side_sum(field):
    wide = jnp.pad(field, [(0, 0)] * (field.ndim - 2) + [(1, 1), (1, 1)])
    total = wide[..., 2:, 1:-1] + wide[..., :-2, 1:-1]
    return total + wide[..., 1:-1, 2:] + wide[..., 1:-1, :-2] - 6.0 * field


def hold(*values):
    return lax.optimization_barrier(values)


def local(forward_states, kappa, courant, direction, obs_index, obs_weight):
    states = forward_states[0, :, 0]
    kappa, courant, direction = kappa[0], courant[0], direction[0]
    steps, rows, columns = states.shape
    slabs = lax.axis_size("grid")
    scens = lax.axis_size("scen")
    even = lax.axis_index("grid") % 2 == 0
    mine = lax.axis_index("scen")

    near = [(g, g ^ 1) for g in range(slabs)]
    far = [(g, g - 1 if g % 2 == 0 else g + 1) for g in range(slabs)]
    far = [(g, h) for g, h in far if 0 <= h < slabs]

    def across(field):
        return lax.ppermute(field, "grid", far)

    def beside(field):
        return lax.ppermute(field, "grid", near)

    overs = [across(states[0])]
    nears = beside(states)
    (later,) = hold(states)
    for step in range(1, steps):
        overs.append(across(later[step]))

    far_gain = jnp.where(even, kappa + courant, kappa)
    near_gain = jnp.where(even, kappa, kappa + courant)
    pull = source_gain * direction
    far_gain, near_gain, pull = hold(far_gain, near_gain, pull)

    inner = [nears[k] + side_sum(later[k]) for k in range(steps)]
    inner = list(hold(*inner))
    laps = [overs[k] + inner[k] for k in range(steps)]

    weights = weight_field(obs_index, obs_weight, rows, columns)

    tangent = pull * laps[0]
    for step in range(1, steps):
        over = across(tangent)
        side = beside(tangent)
        base = tangent + kappa * side_sum(tangent) - courant * tangent + pull * laps[step]
        (base,) = hold(base)
        (base,) = hold(base + near_gain * side)
        tangent = base + far_gain * over

    adjoint = tangent * weights
    partial_value = None
    for step in range(steps - 2, -1, -1):
        over = across(far_gain * adjoint)
        side = beside(near_gain * adjoint)
        term = source_gain * laps[step + 1] * adjoint
        partial_value = term if partial_value is None else partial_value + term
        base = adjoint + side_sum(kappa * adjoint) - courant * adjoint
        base, partial_value = hold(base, partial_value)
        (base,) = hold(base + side)
        if step:
            adjoint = base + over
    last = source_gain * laps[0]
    last, rest = hold(last, partial_value + last * base)
    partial_value = rest + last * over

    share = rows // scens
    pieces = lax.all_to_all(partial_value, "scen", 0, 0, tiled=True)

    own = lax.dynamic_slice_in_dim(direction, mine * share, share, 0)
    tall = jnp.pad(direction, ((1, 1), (0, 0)))
    tall = lax.dynamic_slice_in_dim(tall, mine * share, share + 2, 0)
    lap = across(own) + beside(own) + side_sum(tall)[1:-1]
    prior = prior_gain * (own - prior_reach * lap)
    (prior,) = hold(prior)
    return (jnp.sum(pieces.reshape(scens, share, columns), 0) + prior)[None]


def solution(mesh):
    return jax.shard_map(
        local,
        mesh=mesh,
        in_specs=(
            P("scen", None, "grid", None, None),
            P("grid", None, None),
            P("grid", None, None),
            P("grid", None, None),
            P("scen", "grid"),
            P("scen", "grid"),
        ),
        out_specs=P("grid", "scen", None),
        check_vma=False,
    )
```

```python
import jax
import jax.numpy as jnp
from jax import lax
from jax.experimental import pallas as pl
from jax.experimental.pallas import tpu as pltpu
from jax.sharding import PartitionSpec as P


source_gain = 0.2
prior_gain = 0.5
prior_reach = 0.1


def weight_kernel(index_ref, weight_ref, field_ref):
    rows, columns = field_ref.shape
    chunk = index_ref.shape[1]

    @pl.when(pl.program_id(0) == 0)
    def _():
        field_ref[...] = jnp.zeros_like(field_ref)

    index = index_ref[...]
    row = index // columns
    column = index - row * columns
    left = weight_ref[...]
    row_hit = lax.broadcasted_iota(jnp.int32, (rows, chunk), 0) == row
    column_hit = lax.broadcasted_iota(jnp.int32, (columns, chunk), 0) == column
    column_one = jnp.where(column_hit, 1.0, 0.0).astype(jnp.bfloat16)
    for _ in range(3):
        part = left.astype(jnp.bfloat16).astype(jnp.float32)
        left = left - part
        row_part = jnp.where(row_hit, part, 0.0).astype(jnp.bfloat16)
        field_ref[...] += lax.dot_general(
            row_part, column_one, (((1,), (1,)), ((), ())), preferred_element_type=jnp.float32
        )


def weight_field(index, weight, rows, columns):
    count = index.shape[1]
    chunk = 1024
    return pl.pallas_call(
        weight_kernel,
        grid=(count // chunk,),
        in_specs=[pl.BlockSpec((1, chunk), lambda i: (0, i))] * 2,
        out_specs=pl.BlockSpec((rows, columns), lambda i: (0, 0)),
        out_shape=jax.ShapeDtypeStruct((rows, columns), jnp.float32),
        compiler_params=pltpu.CompilerParams(vmem_limit_bytes=24 << 20),
        cost_estimate=pl.CostEstimate(
            flops=6 * rows * columns * count, bytes_accessed=4 * rows * columns, transcendentals=0
        ),
        name="weight_field",
    )(index, weight)


def side_sum(field):
    wide = jnp.pad(field, [(0, 0)] * (field.ndim - 2) + [(1, 1), (1, 1)])
    total = wide[..., 2:, 1:-1] + wide[..., :-2, 1:-1]
    return total + wide[..., 1:-1, 2:] + wide[..., 1:-1, :-2] - 6.0 * field


def hold(*values):
    return lax.optimization_barrier(values)


def local(forward_states, kappa, courant, direction, obs_index, obs_weight):
    states = forward_states[0, :, 0]
    kappa, courant, direction = kappa[0], courant[0], direction[0]
    steps, rows, columns = states.shape
    slabs = lax.axis_size("grid")
    scens = lax.axis_size("scen")
    share = rows // scens
    even = (lax.axis_index("grid") & 1) == 0
    first = (lax.axis_index("scen") * share).astype(jnp.uint32)

    near = [(g, g ^ 1) for g in range(slabs)]
    far = [(g, g - 1 if g % 2 == 0 else g + 1) for g in range(slabs)]
    far = [(g, h) for g, h in far if 0 <= h < slabs]

    def across(field):
        return lax.ppermute(field, "grid", far)

    def beside(field):
        return lax.ppermute(field, "grid", near)

    states, even, first = hold(states, even, first)
    over = across(states[0])
    nears = beside(states)
    (later,) = hold(states)
    own = lax.dynamic_slice(direction, (first, jnp.uint32(0)), (share, columns))
    sent, own = hold(jnp.concatenate([later[1], own]), own)
    (later,) = hold(later)
    fields = [states[0], sent[:rows], later[2], later[3]]
    fields[2:] = hold(*fields[2:])
    arrived = across(sent)
    overs = [over, arrived[:rows]] + [across(fields[k]) for k in (2, 3)]
    over_own = arrived[rows:]

    far_gain = jnp.where(even, kappa + courant, kappa)
    near_gain = jnp.where(even, kappa, kappa + courant)
    far_gain, near_gain = hold(far_gain, near_gain)

    def lap_of(step):
        return source_gain * (overs[step] + nears[step] + side_sum(fields[step]))

    weights = weight_field(obs_index, obs_weight, rows, columns)

    (inner,) = hold(nears[0] + side_sum(fields[0]))
    laps = [source_gain * (inner + over)]
    tangent = direction * laps[0]
    tangent, laps[0] = hold(tangent, laps[0])
    for step in range(1, steps):
        over = across(tangent)
        if step == 1:
            side = beside(jnp.concatenate([tangent, own]))
            side, side_own = side[:rows], side[rows:]
        else:
            side = beside(tangent)
        laps.append(lap_of(step))
        base = tangent + kappa * side_sum(tangent) - courant * tangent + direction * laps[step]
        base, laps[step] = hold(base, laps[step])
        (base,) = hold(base + near_gain * side)
        tangent = base + far_gain * over

    adjoint = tangent * weights
    partial_value = None
    for step in range(steps - 2, -1, -1):
        over = across(far_gain * adjoint)
        side = beside(near_gain * adjoint)
        term = laps[step + 1] * adjoint
        partial_value = term if partial_value is None else partial_value + term
        base = adjoint + side_sum(kappa * adjoint) - courant * adjoint
        base, partial_value = hold(base, partial_value)
        (base,) = hold(base + side)
        if step:
            adjoint = base + over
    (rest,) = hold(partial_value + laps[0] * base)
    partial_value = rest + laps[0] * over

    pieces = lax.all_to_all(partial_value, "scen", 0, 0, tiled=True)

    tall = jnp.pad(direction, ((1, 1), (0, 0)))
    tall = lax.dynamic_slice(tall, (first, jnp.uint32(0)), (share + 2, columns))
    lap = over_own + side_own + side_sum(tall)[1:-1]
    (prior,) = hold(prior_gain * (own - prior_reach * lap))
    return (jnp.sum(pieces.reshape(scens, share, columns), 0) + prior)[None]


def solution(mesh):
    return jax.shard_map(
        local,
        mesh=mesh,
        in_specs=(
            P("scen", None, "grid", None, None),
            P("grid", None, None),
            P("grid", None, None),
            P("grid", None, None),
            P("scen", "grid"),
            P("scen", "grid"),
        ),
        out_specs=P("grid", "scen", None),
        check_vma=False,
    )
```

```python
import jax
import jax.numpy as jnp
from jax import lax
from jax.experimental import pallas as pl
from jax.experimental.pallas import tpu as pltpu
from jax.sharding import PartitionSpec as P


source_gain = 0.2
prior_gain = 0.5
prior_reach = 0.1


def weight_kernel(index_ref, weight_ref, field_ref):
    rows, columns = field_ref.shape
    chunk = index_ref.shape[1]

    @pl.when(pl.program_id(0) == 0)
    def _():
        field_ref[...] = jnp.zeros_like(field_ref)

    index = index_ref[...]
    row = index // columns
    column = index - row * columns
    left = weight_ref[...]
    row_hit = lax.broadcasted_iota(jnp.int32, (rows, chunk), 0) == row
    column_hit = lax.broadcasted_iota(jnp.int32, (columns, chunk), 0) == column
    column_one = jnp.where(column_hit, 1.0, 0.0).astype(jnp.bfloat16)
    for _ in range(3):
        part = left.astype(jnp.bfloat16).astype(jnp.float32)
        left = left - part
        row_part = jnp.where(row_hit, part, 0.0).astype(jnp.bfloat16)
        field_ref[...] += lax.dot_general(
            row_part, column_one, (((1,), (1,)), ((), ())), preferred_element_type=jnp.float32
        )


def weight_field(index, weight, rows, columns):
    count = index.shape[1]
    chunk = 1024
    return pl.pallas_call(
        weight_kernel,
        grid=(count // chunk,),
        in_specs=[pl.BlockSpec((1, chunk), lambda i: (0, i))] * 2,
        out_specs=pl.BlockSpec((rows, columns), lambda i: (0, 0)),
        out_shape=jax.ShapeDtypeStruct((rows, columns), jnp.float32),
        compiler_params=pltpu.CompilerParams(vmem_limit_bytes=24 << 20),
        cost_estimate=pl.CostEstimate(
            flops=6 * rows * columns * count, bytes_accessed=4 * rows * columns, transcendentals=0
        ),
        name="weight_field",
    )(index, weight)


def side_sum(field):
    wide = jnp.pad(field, [(0, 0)] * (field.ndim - 2) + [(1, 1), (1, 1)])
    total = wide[..., 2:, 1:-1] + wide[..., :-2, 1:-1]
    return total + wide[..., 1:-1, 2:] + wide[..., 1:-1, :-2] - 6.0 * field


def hold(*values):
    return lax.optimization_barrier(values)


def local(forward_states, kappa, courant, direction, obs_index, obs_weight):
    states = forward_states[0, :, 0]
    kappa, courant, direction = kappa[0], courant[0], direction[0]
    steps, rows, columns = states.shape
    slabs = lax.axis_size("grid")
    scens = lax.axis_size("scen")
    share = rows // scens
    even = (lax.axis_index("grid") & 1) == 0
    first = (lax.axis_index("scen") * share).astype(jnp.uint32)

    near = [(g, g ^ 1) for g in range(slabs)]
    far = [(g, g - 1 if g % 2 == 0 else g + 1) for g in range(slabs)]
    far = [(g, h) for g, h in far if 0 <= h < slabs]

    def across(field):
        return lax.ppermute(field, "grid", far)

    def beside(field):
        return lax.ppermute(field, "grid", near)

    upper = (lax.axis_index("scen") & 1) == 1
    states, even, first, upper = hold(states, even, first, upper)
    over = across(states[0])
    nears = beside(states)
    (later,) = hold(states)
    fields = [states[0]]
    for step in range(1, steps):
        (field,) = hold(later[step])
        fields.append(field)
        (later,) = hold(later)
    own = lax.dynamic_slice(direction, (first, jnp.uint32(0)), (share, columns))
    sent, own = hold(jnp.concatenate([fields[2], own]), own)
    arrived = across(sent)
    overs = [over, across(fields[1]), arrived[:rows], across(fields[3])]
    over_own = arrived[rows:]

    far_gain = jnp.where(even, kappa + courant, kappa)
    near_gain = jnp.where(even, kappa, kappa + courant)
    far_gain, near_gain = hold(far_gain, near_gain)

    def lap_of(step):
        return source_gain * (overs[step] + nears[step] + side_sum(fields[step]))

    weights = weight_field(obs_index, obs_weight, rows, columns)

    (inner,) = hold(nears[0] + side_sum(fields[0]))
    laps = [source_gain * (inner + over)]
    tangent = direction * laps[0]
    tangent, laps[0] = hold(tangent, laps[0])
    for step in range(1, steps):
        over = across(tangent)
        if step == 2:
            side = beside(jnp.concatenate([tangent, own]))
            side, side_own = side[:rows], side[rows:]
        else:
            side = beside(tangent)
        laps.append(lap_of(step))
        base = tangent + kappa * side_sum(tangent) - courant * tangent
        base = base + direction * laps[step]
        base, laps[step] = hold(base, laps[step])
        (base,) = hold(base + near_gain * side)
        tangent = base + far_gain * over

    adjoint = tangent * weights
    partial_value = None
    for step in range(steps - 2, -1, -1):
        over = across(far_gain * adjoint)
        side = beside(near_gain * adjoint)
        term = laps[step + 1] * adjoint
        partial_value = term if partial_value is None else partial_value + term
        base = adjoint + side_sum(kappa * adjoint) - courant * adjoint
        base, partial_value = hold(base, partial_value)
        (base,) = hold(base + side)
        if step:
            adjoint = base + over
    (rest,) = hold(partial_value + laps[0] * base)
    partial_value = rest + laps[0] * over

    groups = [list(range(side, scens, 2)) for side in range(2)]
    pieces = lax.all_to_all(
        partial_value, "scen", 0, 0, axis_index_groups=groups, tiled=True
    )

    tall = jnp.pad(direction, ((1, 1), (0, 0)))
    tall = lax.dynamic_slice(tall, (first, jnp.uint32(0)), (share + 2, columns))
    lap = over_own + side_own + side_sum(tall)[1:-1]
    (prior,) = hold(prior_gain * (own - prior_reach * lap))
    pieces = pieces.reshape(scens // 2, 2, share, columns)
    kept = jnp.where(upper, pieces[:, 1], pieces[:, 0])
    other = jnp.where(upper, pieces[:, 0], pieces[:, 1])
    (other,) = hold(jnp.sum(other, 0))
    other = lax.ppermute(other, "scen", [(s, s ^ 1) for s in range(scens)])
    (kept,) = hold(jnp.sum(kept, 0) + prior)
    return (kept + other)[None]


def solution(mesh):
    return jax.shard_map(
        local,
        mesh=mesh,
        in_specs=(
            P("scen", None, "grid", None, None),
            P("grid", None, None),
            P("grid", None, None),
            P("grid", None, None),
            P("scen", "grid"),
            P("scen", "grid"),
        ),
        out_specs=P("grid", "scen", None),
        check_vma=False,
    )
```

```python
import jax
import jax.numpy as jnp
from jax import lax
from jax.experimental import pallas as pl
from jax.experimental.pallas import tpu as pltpu
from jax.sharding import PartitionSpec as P


source_gain = 0.2
prior_gain = 0.5
prior_reach = 0.1


def weight_kernel(index_ref, weight_ref, field_ref):
    rows, columns = field_ref.shape
    chunk = index_ref.shape[1]

    @pl.when(pl.program_id(0) == 0)
    def _():
        field_ref[...] = jnp.zeros_like(field_ref)

    index = index_ref[...]
    row = index // columns
    column = index - row * columns
    left = weight_ref[...]
    row_hit = lax.broadcasted_iota(jnp.int32, (rows, chunk), 0) == row
    column_hit = lax.broadcasted_iota(jnp.int32, (columns, chunk), 0) == column
    column_one = jnp.where(column_hit, 1.0, 0.0).astype(jnp.bfloat16)
    for _ in range(3):
        part = left.astype(jnp.bfloat16).astype(jnp.float32)
        left = left - part
        row_part = jnp.where(row_hit, part, 0.0).astype(jnp.bfloat16)
        field_ref[...] += lax.dot_general(
            row_part, column_one, (((1,), (1,)), ((), ())), preferred_element_type=jnp.float32
        )


def weight_field(index, weight, rows, columns):
    count = index.shape[1]
    chunk = 1024
    return pl.pallas_call(
        weight_kernel,
        grid=(count // chunk,),
        in_specs=[pl.BlockSpec((1, chunk), lambda i: (0, i))] * 2,
        out_specs=pl.BlockSpec((rows, columns), lambda i: (0, 0)),
        out_shape=jax.ShapeDtypeStruct((rows, columns), jnp.float32),
        compiler_params=pltpu.CompilerParams(vmem_limit_bytes=24 << 20),
        cost_estimate=pl.CostEstimate(
            flops=6 * rows * columns * count, bytes_accessed=4 * rows * columns, transcendentals=0
        ),
        name="weight_field",
    )(index, weight)


def side_sum(field):
    wide = jnp.pad(field, [(0, 0)] * (field.ndim - 2) + [(1, 1), (1, 1)])
    total = wide[..., 2:, 1:-1] + wide[..., :-2, 1:-1]
    return total + wide[..., 1:-1, 2:] + wide[..., 1:-1, :-2] - 6.0 * field


def hold(*values):
    return lax.optimization_barrier(values)


def local(forward_states, kappa, courant, direction, obs_index, obs_weight):
    states = forward_states[0, :, 0]
    kappa, courant, direction = kappa[0], courant[0], direction[0]
    steps, rows, columns = states.shape
    slabs = lax.axis_size("grid")
    scens = lax.axis_size("scen")
    share = rows // scens
    even = (lax.axis_index("grid") & 1) == 0
    first = (lax.axis_index("scen") * share).astype(jnp.uint32)

    near = [(g, g ^ 1) for g in range(slabs)]
    far = [(g, g - 1 if g % 2 == 0 else g + 1) for g in range(slabs)]
    far = [(g, h) for g, h in far if 0 <= h < slabs]

    def across(field):
        return lax.ppermute(field, "grid", far)

    def beside(field):
        return lax.ppermute(field, "grid", near)

    upper = (lax.axis_index("scen") & 1) == 1
    states, even, first, upper = hold(states, even, first, upper)
    over = across(states[0])
    nears = beside(states)
    (later,) = hold(states)
    fields = [states[0]]
    for step in range(1, steps):
        (field,) = hold(later[step])
        fields.append(field)
        (later,) = hold(later)
    own = lax.dynamic_slice(direction, (first, jnp.uint32(0)), (share, columns))
    sent, own = hold(jnp.concatenate([fields[2], own]), own)
    arrived = across(sent)
    overs = [over, across(fields[1]), arrived[:rows], across(fields[3])]
    over_own = arrived[rows:]

    far_gain = jnp.where(even, kappa + courant, kappa)
    near_gain = jnp.where(even, kappa, kappa + courant)
    far_gain, near_gain = hold(far_gain, near_gain)

    def lap_of(step):
        return source_gain * (overs[step] + nears[step] + side_sum(fields[step]))

    weights = weight_field(obs_index, obs_weight, rows, columns)

    (inner,) = hold(nears[0] + side_sum(fields[0]))
    laps = [source_gain * (inner + over)]
    tangent = direction * laps[0]
    tangent, laps[0] = hold(tangent, laps[0])
    for step in range(1, steps):
        over = across(tangent)
        if step == 2:
            side = beside(jnp.concatenate([tangent, own]))
            side, side_own = side[:rows], side[rows:]
        else:
            side = beside(tangent)
        laps.append(lap_of(step))
        base = tangent + kappa * side_sum(tangent) - courant * tangent
        base = base + direction * laps[step]
        base, laps[step] = hold(base, laps[step])
        (base,) = hold(base + near_gain * side)
        tangent = base + far_gain * over

    adjoint = tangent * weights
    lap_over = across(laps[0])
    partial_value = None
    for step in range(steps - 2, -1, -1):
        sent = far_gain * adjoint
        if step:
            over = across(sent)
        side = beside(near_gain * adjoint)
        term = laps[step + 1] * adjoint
        partial_value = term if partial_value is None else partial_value + term
        base = adjoint + side_sum(kappa * adjoint) - courant * adjoint
        base, partial_value = hold(base, partial_value)
        if step:
            (base,) = hold(base + side)
            adjoint = base + over
    product, rest = hold(lap_over * sent, partial_value + laps[0] * base)
    value = rest + laps[0] * side
    value = jnp.concatenate(
        [jnp.where(even, product, value), jnp.where(even, value, product)]
    )

    pairs = [(g, (g + 1) % slabs) for g in range(1, slabs, 2)]
    groups = [
        [(2 * x + side) * slabs + g for g in pair for x in range(scens // 2)]
        for pair in pairs
        for side in range(2)
    ]
    pieces = lax.all_to_all(
        value, ("scen", "grid"), 0, 0, axis_index_groups=groups, tiled=True
    )

    tall = jnp.pad(direction, ((1, 1), (0, 0)))
    tall = lax.dynamic_slice(tall, (first, jnp.uint32(0)), (share + 2, columns))
    lap = over_own + side_own + side_sum(tall)[1:-1]
    (prior,) = hold(prior_gain * (own - prior_reach * lap))
    pieces = pieces.reshape(scens, 2, share, columns)
    kept = jnp.where(upper, pieces[:, 1], pieces[:, 0])
    other = jnp.where(upper, pieces[:, 0], pieces[:, 1])
    (other,) = hold(jnp.sum(other, 0))
    other = lax.ppermute(other, "scen", [(s, s ^ 1) for s in range(scens)])
    (kept,) = hold(jnp.sum(kept, 0) + prior)
    return (kept + other)[None]


def solution(mesh):
    return jax.shard_map(
        local,
        mesh=mesh,
        in_specs=(
            P("scen", None, "grid", None, None),
            P("grid", None, None),
            P("grid", None, None),
            P("grid", None, None),
            P("scen", "grid"),
            P("scen", "grid"),
        ),
        out_specs=P("grid", "scen", None),
        check_vma=False,
    )
```

```python
import jax
import jax.numpy as jnp
from jax import lax
from jax.experimental import pallas as pl
from jax.experimental.pallas import tpu as pltpu
from jax.sharding import PartitionSpec as P


source_gain = 0.2
prior_gain = 0.5
prior_reach = 0.1


def weight_kernel(index_ref, weight_ref, field_ref):
    rows, columns = field_ref.shape
    chunk = index_ref.shape[1]

    @pl.when(pl.program_id(0) == 0)
    def _():
        field_ref[...] = jnp.zeros_like(field_ref)

    index = index_ref[...]
    row = index // columns
    column = index - row * columns
    left = weight_ref[...]
    row_hit = lax.broadcasted_iota(jnp.int32, (rows, chunk), 0) == row
    column_hit = lax.broadcasted_iota(jnp.int32, (columns, chunk), 0) == column
    column_one = jnp.where(column_hit, 1.0, 0.0).astype(jnp.bfloat16)
    for _ in range(3):
        part = left.astype(jnp.bfloat16).astype(jnp.float32)
        left = left - part
        row_part = jnp.where(row_hit, part, 0.0).astype(jnp.bfloat16)
        field_ref[...] += lax.dot_general(
            row_part, column_one, (((1,), (1,)), ((), ())), preferred_element_type=jnp.float32
        )


def weight_field(index, weight, rows, columns):
    count = index.shape[1]
    chunk = 1024
    return pl.pallas_call(
        weight_kernel,
        grid=(count // chunk,),
        in_specs=[pl.BlockSpec((1, chunk), lambda i: (0, i))] * 2,
        out_specs=pl.BlockSpec((rows, columns), lambda i: (0, 0)),
        out_shape=jax.ShapeDtypeStruct((rows, columns), jnp.float32),
        compiler_params=pltpu.CompilerParams(vmem_limit_bytes=24 << 20),
        cost_estimate=pl.CostEstimate(
            flops=6 * rows * columns * count, bytes_accessed=4 * rows * columns, transcendentals=0
        ),
        name="weight_field",
    )(index, weight)


def side_sum(field):
    wide = jnp.pad(field, [(0, 0)] * (field.ndim - 2) + [(1, 1), (1, 1)])
    total = wide[..., 2:, 1:-1] + wide[..., :-2, 1:-1]
    return total + wide[..., 1:-1, 2:] + wide[..., 1:-1, :-2] - 6.0 * field


def hold(*values):
    return lax.optimization_barrier(values)


def local(forward_states, kappa, courant, direction, obs_index, obs_weight):
    states = forward_states[0, :, 0]
    kappa, courant, direction = kappa[0], courant[0], direction[0]
    steps, rows, columns = states.shape
    slabs = lax.axis_size("grid")
    scens = lax.axis_size("scen")
    share = rows // scens
    even = (lax.axis_index("grid") & 1) == 0
    first = (lax.axis_index("scen") * share).astype(jnp.uint32)

    near = [(g, g ^ 1) for g in range(slabs)]
    far = [(g, g - 1 if g % 2 == 0 else g + 1) for g in range(slabs)]
    far = [(g, h) for g, h in far if 0 <= h < slabs]

    def across(field):
        return lax.ppermute(field, "grid", far)

    def beside(field):
        return lax.ppermute(field, "grid", near)

    upper = (lax.axis_index("scen") & 1) == 1
    states, even, first, upper = hold(states, even, first, upper)
    over = across(states[0])
    nears = beside(states)
    (later,) = hold(states)
    fields = [states[0]]
    for step in range(1, steps):
        (field,) = hold(later[step])
        fields.append(field)
        (later,) = hold(later)
    own = lax.dynamic_slice(direction, (first, jnp.uint32(0)), (share, columns))
    sent, own = hold(jnp.concatenate([fields[2], own]), own)
    arrived = across(sent)
    overs = [over, across(fields[1]), arrived[:rows], across(fields[3])]
    over_own = arrived[rows:]

    far_gain = jnp.where(even, kappa + courant, kappa)
    near_gain = jnp.where(even, kappa, kappa + courant)
    far_gain, near_gain = hold(far_gain, near_gain)

    def lap_of(step):
        return source_gain * (overs[step] + nears[step] + side_sum(fields[step]))

    gain_pair = far_gain * across(far_gain)

    weights = weight_field(obs_index, obs_weight, rows, columns)

    (inner,) = hold(nears[0] + side_sum(fields[0]))
    laps = [source_gain * (inner + over)]
    tangent = direction * laps[0]
    tangent, laps[0] = hold(tangent, laps[0])
    for step in range(1, steps):
        over = across(tangent)
        if step == 2:
            side = beside(jnp.concatenate([tangent, own]))
            side, side_own = side[:rows], side[rows:]
        else:
            side = beside(tangent)
        laps.append(lap_of(step))
        base = tangent + kappa * side_sum(tangent) - courant * tangent
        base = base + direction * laps[step]
        base, laps[step] = hold(base, laps[step])
        (base,) = hold(base + near_gain * side)
        tangent = base + far_gain * over

    def settled(field):
        side = beside(near_gain * field)
        base = field + side_sum(kappa * field) - courant * field
        (base,) = hold(base)
        return hold(base + side)[0]

    adjoint, sent = hold(tangent * weights, far_gain * (tangent * weights))
    over = across(sent)
    ready = settled(adjoint)
    sent, ready, before = hold(far_gain * ready, ready, adjoint)
    early = across(sent)
    echo, partial_value = hold(gain_pair * before, laps[3] * before)
    (adjoint,) = hold(ready + over)
    ready = settled(adjoint)
    sent, ready, before = hold(far_gain * ready, ready, adjoint)
    later = across(sent)
    ready, echo, partial_value = hold(
        ready + echo, gain_pair * before, partial_value + laps[2] * before
    )
    (adjoint,) = hold(ready + early)
    ready = settled(adjoint)
    (rest,) = hold(partial_value + laps[1] * adjoint + laps[0] * (ready + echo))
    partial_value = rest + laps[0] * later

    groups = [list(range(side, scens, 2)) for side in range(2)]
    pieces = lax.all_to_all(
        partial_value, "scen", 0, 0, axis_index_groups=groups, tiled=True
    )

    tall = jnp.pad(direction, ((1, 1), (0, 0)))
    tall = lax.dynamic_slice(tall, (first, jnp.uint32(0)), (share + 2, columns))
    lap = over_own + side_own + side_sum(tall)[1:-1]
    (prior,) = hold(prior_gain * (own - prior_reach * lap))
    pieces = pieces.reshape(scens // 2, 2, share, columns)
    kept = jnp.where(upper, pieces[:, 1], pieces[:, 0])
    other = jnp.where(upper, pieces[:, 0], pieces[:, 1])
    (other,) = hold(jnp.sum(other, 0))
    other = lax.ppermute(other, "scen", [(s, s ^ 1) for s in range(scens)])
    (kept,) = hold(jnp.sum(kept, 0) + prior)
    return (kept + other)[None]


def solution(mesh):
    return jax.shard_map(
        local,
        mesh=mesh,
        in_specs=(
            P("scen", None, "grid", None, None),
            P("grid", None, None),
            P("grid", None, None),
            P("grid", None, None),
            P("scen", "grid"),
            P("scen", "grid"),
        ),
        out_specs=P("grid", "scen", None),
        check_vma=False,
    )
```

```python
import jax
import jax.numpy as jnp
from jax import lax
from jax.experimental import pallas as pl
from jax.experimental.pallas import tpu as pltpu
from jax.sharding import PartitionSpec as P


source_gain = 0.2
prior_gain = 0.5
prior_reach = 0.1


def weight_kernel(index_ref, weight_ref, field_ref):
    rows, columns = field_ref.shape
    chunk = index_ref.shape[1]

    @pl.when(pl.program_id(0) == 0)
    def _():
        field_ref[...] = jnp.zeros_like(field_ref)

    index = index_ref[...]
    row = index // columns
    column = index - row * columns
    left = weight_ref[...]
    row_hit = lax.broadcasted_iota(jnp.int32, (rows, chunk), 0) == row
    column_hit = lax.broadcasted_iota(jnp.int32, (columns, chunk), 0) == column
    column_one = jnp.where(column_hit, 1.0, 0.0).astype(jnp.bfloat16)
    for _ in range(3):
        part = left.astype(jnp.bfloat16).astype(jnp.float32)
        left = left - part
        row_part = jnp.where(row_hit, part, 0.0).astype(jnp.bfloat16)
        field_ref[...] += lax.dot_general(
            row_part, column_one, (((1,), (1,)), ((), ())), preferred_element_type=jnp.float32
        )


def weight_field(index, weight, rows, columns, part, parts):
    count = index.shape[1] // parts
    chunk = count // 2
    return pl.pallas_call(
        weight_kernel,
        grid=(2,),
        in_specs=[pl.BlockSpec((1, chunk), lambda i: (0, 2 * part + i))] * 2,
        out_specs=pl.BlockSpec((rows, columns), lambda i: (0, 0)),
        out_shape=jax.ShapeDtypeStruct((rows, columns), jnp.float32),
        compiler_params=pltpu.CompilerParams(vmem_limit_bytes=24 << 20),
        cost_estimate=pl.CostEstimate(
            flops=6 * rows * columns * count, bytes_accessed=4 * rows * columns, transcendentals=0
        ),
        name="weight_field",
    )(index, weight)


def side_sum(field):
    wide = jnp.pad(field, [(0, 0)] * (field.ndim - 2) + [(1, 1), (1, 1)])
    total = wide[..., 2:, 1:-1] + wide[..., :-2, 1:-1]
    return total + wide[..., 1:-1, 2:] + wide[..., 1:-1, :-2] - 6.0 * field


def hold(*values):
    return lax.optimization_barrier(values)


def local(forward_states, kappa, courant, direction, obs_index, obs_weight):
    states = forward_states[0, :, 0]
    kappa, courant, direction = kappa[0], courant[0], direction[0]
    steps, rows, columns = states.shape
    slabs = lax.axis_size("grid")
    scens = lax.axis_size("scen")
    share = rows // scens
    even = (lax.axis_index("grid") & 1) == 0
    first = (lax.axis_index("scen") * share).astype(jnp.uint32)

    near = [(g, g ^ 1) for g in range(slabs)]
    far = [(g, g - 1 if g % 2 == 0 else g + 1) for g in range(slabs)]
    far = [(g, h) for g, h in far if 0 <= h < slabs]

    def across(field):
        return lax.ppermute(field, "grid", far)

    def beside(field):
        return lax.ppermute(field, "grid", near)

    upper = (lax.axis_index("scen") & 1) == 1
    states, even, first, upper = hold(states, even, first, upper)
    over = across(states[0])
    nears = beside(states)
    (later,) = hold(states)
    fields = [states[0]]
    for step in range(1, steps):
        (field,) = hold(later[step])
        fields.append(field)
        (later,) = hold(later)
    own = lax.dynamic_slice(direction, (first, jnp.uint32(0)), (share, columns))
    sent, own = hold(jnp.concatenate([fields[2], own]), own)
    arrived = across(sent)
    overs = [over, across(fields[1]), arrived[:rows], across(fields[3])]
    over_own = arrived[rows:]

    far_gain = jnp.where(even, kappa + courant, kappa)
    near_gain = jnp.where(even, kappa, kappa + courant)
    far_gain, near_gain = hold(far_gain, near_gain)

    def lap_of(step):
        return source_gain * (overs[step] + nears[step] + side_sum(fields[step]))

    gain_pair = far_gain * across(far_gain)

    weights = weight_field(obs_index, obs_weight, rows, columns, 0, 2)
    more_weights = weight_field(obs_index, obs_weight, rows, columns, 1, 2)

    (inner,) = hold(nears[0] + side_sum(fields[0]))
    laps = [source_gain * (inner + over)]
    tangent = direction * laps[0]
    tangent, laps[0] = hold(tangent, laps[0])
    for step in range(1, steps):
        over = across(tangent)
        if step == 2:
            side = beside(jnp.concatenate([tangent, own]))
            side, side_own = side[:rows], side[rows:]
        else:
            side = beside(tangent)
        laps.append(lap_of(step))
        base = tangent + kappa * side_sum(tangent) - courant * tangent
        base = base + direction * laps[step]
        base, laps[step] = hold(base, laps[step])
        (base,) = hold(base + near_gain * side)
        tangent = base + far_gain * over

    def settled(field):
        side = beside(near_gain * field)
        base = field + side_sum(kappa * field) - courant * field
        (base,) = hold(base)
        return hold(base + side)[0]

    adjoint = tangent * (weights + more_weights)
    adjoint, sent = hold(adjoint, far_gain * adjoint)
    over = across(sent)
    ready = settled(adjoint)
    sent, ready, before = hold(far_gain * ready, ready, adjoint)
    early = across(sent)
    echo, partial_value = hold(gain_pair * before, laps[3] * before)
    (adjoint,) = hold(ready + over)
    ready = settled(adjoint)
    sent, ready, before = hold(far_gain * ready, ready, adjoint)
    later = across(sent)
    ready, echo, partial_value = hold(
        ready + echo, gain_pair * before, partial_value + laps[2] * before
    )
    (adjoint,) = hold(ready + early)
    ready = settled(adjoint)
    (rest,) = hold(partial_value + laps[1] * adjoint + laps[0] * (ready + echo))
    partial_value = rest + laps[0] * later

    groups = [list(range(side, scens, 2)) for side in range(2)]
    pieces = lax.all_to_all(
        partial_value, "scen", 0, 0, axis_index_groups=groups, tiled=True
    )

    tall = jnp.pad(direction, ((1, 1), (0, 0)))
    tall = lax.dynamic_slice(tall, (first, jnp.uint32(0)), (share + 2, columns))
    lap = over_own + side_own + side_sum(tall)[1:-1]
    (prior,) = hold(prior_gain * (own - prior_reach * lap))
    pieces = pieces.reshape(scens // 2, 2, share, columns)
    kept = jnp.where(upper, pieces[:, 1], pieces[:, 0])
    other = jnp.where(upper, pieces[:, 0], pieces[:, 1])
    (other,) = hold(jnp.sum(other, 0))
    other = lax.ppermute(other, "scen", [(s, s ^ 1) for s in range(scens)])
    (kept,) = hold(jnp.sum(kept, 0) + prior)
    return (kept + other)[None]


def solution(mesh):
    return jax.shard_map(
        local,
        mesh=mesh,
        in_specs=(
            P("scen", None, "grid", None, None),
            P("grid", None, None),
            P("grid", None, None),
            P("grid", None, None),
            P("scen", "grid"),
            P("scen", "grid"),
        ),
        out_specs=P("grid", "scen", None),
        check_vma=False,
    )
```

```python
import jax
import jax.numpy as jnp
from jax import lax
from jax.experimental import pallas as pl
from jax.experimental.pallas import tpu as pltpu
from jax.sharding import PartitionSpec as P


source_gain = 0.2
prior_gain = 0.5
prior_reach = 0.1


def weight_kernel(index_ref, weight_ref, field_ref):
    rows, columns = field_ref.shape
    chunk = index_ref.shape[1]

    @pl.when(pl.program_id(0) == 0)
    def _():
        field_ref[...] = jnp.zeros_like(field_ref)

    index = index_ref[...]
    row = index // columns
    column = index - row * columns
    left = weight_ref[...]
    row_hit = lax.broadcasted_iota(jnp.int32, (rows, chunk), 0) == row
    column_hit = lax.broadcasted_iota(jnp.int32, (columns, chunk), 0) == column
    column_one = jnp.where(column_hit, 1.0, 0.0).astype(jnp.bfloat16)
    for _ in range(3):
        part = left.astype(jnp.bfloat16).astype(jnp.float32)
        left = left - part
        row_part = jnp.where(row_hit, part, 0.0).astype(jnp.bfloat16)
        field_ref[...] += lax.dot_general(
            row_part, column_one, (((1,), (1,)), ((), ())), preferred_element_type=jnp.float32
        )


def weight_field(index, weight, rows, columns, part, parts):
    count = index.shape[1] // parts
    chunk = count // 2
    return pl.pallas_call(
        weight_kernel,
        grid=(2,),
        in_specs=[pl.BlockSpec((1, chunk), lambda i: (0, 2 * part + i))] * 2,
        out_specs=pl.BlockSpec((rows, columns), lambda i: (0, 0)),
        out_shape=jax.ShapeDtypeStruct((rows, columns), jnp.float32),
        compiler_params=pltpu.CompilerParams(vmem_limit_bytes=24 << 20),
        cost_estimate=pl.CostEstimate(
            flops=6 * rows * columns * count, bytes_accessed=4 * rows * columns, transcendentals=0
        ),
        name="weight_field",
    )(index, weight)


def side_sum(field):
    wide = jnp.pad(field, [(0, 0)] * (field.ndim - 2) + [(1, 1), (1, 1)])
    total = wide[..., 2:, 1:-1] + wide[..., :-2, 1:-1]
    return total + wide[..., 1:-1, 2:] + wide[..., 1:-1, :-2] - 6.0 * field


def hold(*values):
    return lax.optimization_barrier(values)


def local(forward_states, kappa, courant, direction, obs_index, obs_weight):
    states = forward_states[0, :, 0]
    kappa, courant, direction = kappa[0], courant[0], direction[0]
    steps, rows, columns = states.shape
    slabs = lax.axis_size("grid")
    scens = lax.axis_size("scen")
    share = rows // scens
    even = (lax.axis_index("grid") & 1) == 0
    first = (lax.axis_index("scen") * share).astype(jnp.uint32)

    near = [(g, g ^ 1) for g in range(slabs)]
    far = [(g, g - 1 if g % 2 == 0 else g + 1) for g in range(slabs)]
    far = [(g, h) for g, h in far if 0 <= h < slabs]

    def across(field):
        return lax.ppermute(field, "grid", far)

    def beside(field):
        return lax.ppermute(field, "grid", near)

    upper = (lax.axis_index("scen") & 1) == 1
    states, even, first, upper = hold(states, even, first, upper)
    over = across(states[0])
    nears = beside(states)
    (later,) = hold(states)
    fields = [states[0]]
    for step in range(1, steps):
        (field,) = hold(later[step])
        fields.append(field)
        (later,) = hold(later)
    own = lax.dynamic_slice(direction, (first, jnp.uint32(0)), (share, columns))
    sent, own = hold(jnp.concatenate([fields[2], own]), own)
    arrived = across(sent)
    overs = [over, across(fields[1]), arrived[:rows], across(fields[3])]
    over_own = arrived[rows:]

    far_gain = jnp.where(even, kappa + courant, kappa)
    near_gain = jnp.where(even, kappa, kappa + courant)
    far_gain, near_gain = hold(far_gain, near_gain)

    def lap_of(step):
        return source_gain * (overs[step] + nears[step] + side_sum(fields[step]))

    gain_pair = far_gain * across(far_gain)

    weights = weight_field(obs_index, obs_weight, rows, columns, 0, 2)
    more_weights = weight_field(obs_index, obs_weight, rows, columns, 1, 2)

    (inner,) = hold(nears[0] + side_sum(fields[0]))
    laps = [source_gain * (inner + over)]
    tangent = direction * laps[0]
    tangent, laps[0] = hold(tangent, laps[0])
    for step in range(1, steps):
        over = across(tangent)
        if step == 2:
            side = beside(jnp.concatenate([tangent, own]))
            side, side_own = side[:rows], side[rows:]
        else:
            side = beside(tangent)
        laps.append(lap_of(step))
        base = tangent + kappa * side_sum(tangent) - courant * tangent
        base = base + direction * laps[step]
        base, laps[step] = hold(base, laps[step])
        (base,) = hold(base + near_gain * side)
        tangent = base + far_gain * over

    def settled(field):
        weighted = near_gain * field
        base = field + side_sum(kappa * field) - courant * field
        weighted, base = hold(weighted, base)
        return hold(base + beside(weighted))[0]

    adjoint = tangent * (weights + more_weights)
    adjoint, sent = hold(adjoint, far_gain * adjoint)
    over = across(sent)
    ready = settled(adjoint)
    sent, ready, before = hold(far_gain * ready, ready, adjoint)
    early = across(sent)
    echo, partial_value = hold(gain_pair * before, laps[3] * before)
    (adjoint,) = hold(ready + over)
    ready = settled(adjoint)
    sent, ready, before = hold(far_gain * ready, ready, adjoint)
    later = across(sent)
    ready, echo, partial_value = hold(
        ready + echo, gain_pair * before, partial_value + laps[2] * before
    )
    (adjoint,) = hold(ready + early)
    ready = settled(adjoint)
    (rest,) = hold(partial_value + laps[1] * adjoint + laps[0] * (ready + echo))
    partial_value = rest + laps[0] * later

    groups = [list(range(side, scens, 2)) for side in range(2)]
    pieces = lax.all_to_all(
        partial_value, "scen", 0, 0, axis_index_groups=groups, tiled=True
    )

    tall = jnp.pad(direction, ((1, 1), (0, 0)))
    tall = lax.dynamic_slice(tall, (first, jnp.uint32(0)), (share + 2, columns))
    lap = over_own + side_own + side_sum(tall)[1:-1]
    (prior,) = hold(prior_gain * (own - prior_reach * lap))
    pieces = pieces.reshape(scens // 2, 2, share, columns)
    kept = jnp.where(upper, pieces[:, 1], pieces[:, 0])
    other = jnp.where(upper, pieces[:, 0], pieces[:, 1])
    (other,) = hold(jnp.sum(other, 0))
    other = lax.ppermute(other, "scen", [(s, s ^ 1) for s in range(scens)])
    (kept,) = hold(jnp.sum(kept, 0) + prior)
    return (kept + other)[None]


def solution(mesh):
    return jax.shard_map(
        local,
        mesh=mesh,
        in_specs=(
            P("scen", None, "grid", None, None),
            P("grid", None, None),
            P("grid", None, None),
            P("grid", None, None),
            P("scen", "grid"),
            P("scen", "grid"),
        ),
        out_specs=P("grid", "scen", None),
        check_vma=False,
    )
```
